256 devices in a mesh: dp: 16 (over z_lo, y, core), mp: 16 (over x, z_hi).
Axes of the slice: x: 4, y: 4, z: 8 (z_hi: 4, z_lo: 2; z = z_hi * 2 + z_lo), core: 2. Of those that a mesh axis runs over, the one named last changes fastest.
Arguments:
- prompt_states: bfloat16 [16, 1024, 2048], P('dp'), may hold values from -6 to 6
- norm_gain: float32 [2048], replicated, may hold values from 0.25 to 1.75
- query_gain: float32 [128], replicated, may hold values from 0.1 to 1.9
- key_gain: float32 [128], replicated, may hold values from 0.1 to 1.9
- trainer_qkv: float32 [2048, 4096], P(('dp', 'mp')), may hold values from -0.125 to 0.125
- trainer_gate_up: float32 [2048, 12288], P(('dp', 'mp')), may hold values from -0.125 to 0.125
- cache_pages: bfloat16 [16, 16, 512, 2048], P('dp', 'mp')
- cache_lengths: int32 [16], P('dp'), may hold values from 0 to 8192, as said below
- piece_table: int32 [16, 16], P('dp'), may hold values from 0 to 15, each once within a row
Outputs:
- server_qkv: bfloat16 [2048, 6144], P(None, 'mp')
- server_gate_up: bfloat16 [2048, 12288], P(None, 'mp')
- attention_out: bfloat16 [16, 1024, 2048], P('dp', None, 'mp')
The draws below stay inside these ranges and needn't reach their ends.
Inputs may be any that keep to these rules, and one draw needn't show every extreme that they name: `cache_lengths`: 8 prompts continue a cached request and have 1 or more earlier tokens, one of them exactly 8192; the others have 0. `piece_table`: each row holds every piece index once.
All inputs are finite; a program needn't handle non-finite values.
Results may differ from the reference program's by a relative error of at most 0.017.
The reference program's roundings to bfloat16 on the way (of `normed`) count: a program that leaves them out, or rounds other values in their place, can miss the bound.
Values may be sent and summed in bfloat16 or wider, within the bound.
A program may use at most 128 MiB of HBM per device.

```python
import jax
import jax.numpy as jnp
import numpy as np
from jax import lax

D = 2048
HQ = 16
KVH = 8
HD = 128
FF = 6144
PLEN = 1024
PIECE = 512
PROMPTS = 16
SLOTS_G = 16
CACHE_MAX = 8192
QPD = 1
KPD = 1
BW = 384
N_MP = 16


def draw_cache_lengths(key, part):
    first_key = jax.random.fold_in(key, 11)
    second_key = jax.random.fold_in(key, 12)
    order = jax.random.permutation(first_key, PROMPTS)
    drawn = jax.random.randint(second_key, (PROMPTS,), 1, CACHE_MAX + 1)
    drawn = jnp.where(order == 0, CACHE_MAX, drawn)
    return jnp.where(order < PROMPTS // 2, drawn, 0).astype(jnp.int32)


def draw_cache_pages(key, part):
    first_key = jax.random.fold_in(key, 21)
    full_width = 2 * KVH * HD
    drawn = jnp.clip(jax.random.normal(first_key, (PROMPTS, SLOTS_G, PIECE, full_width), jnp.float32), -6.0, 6.0)
    return drawn.astype(jnp.bfloat16)


def levels(own_key, shape, cuts, smallest, top_value):
    def one(dim, parts):
        steps = jax.random.uniform(jax.random.fold_in(jax.random.fold_in(own_key, 6), dim), (parts,), jnp.float32, smallest / len(cuts), top_value / len(cuts))
        return jnp.repeat(jnp.exp(steps), shape[dim] // parts).reshape((-1,) + (1,) * (len(shape) - dim - 1))

    level = one(*cuts[0])
    for cut in cuts[1:]:
        level = level * one(*cut)
    return level


def bell_draw(rng, dims, spread, bound, shards=(), held_as=jnp.bfloat16):
    factor_of = levels(rng, dims, shards, -0.22, 0.18) if shards else 1.0
    result = jax.random.normal(rng, dims, jnp.float32) * spread * factor_of
    return jnp.minimum(jnp.maximum(result, -bound), bound).astype(held_as)


def setup_inputs(seed: int = 0) -> dict:
    streams_of = jax.random.split(jax.random.key(seed), 10)
    return {
        "prompt_states": bell_draw(streams_of[0], (PROMPTS, PLEN, D), 1.0, 6.0, ((0, 16),)),
        "norm_gain": jnp.clip(1.0 + 0.15 * jax.random.normal(streams_of[1], (D,), jnp.float32), 0.25, 1.75),
        "query_gain": jnp.clip(1.0 + 0.18 * jax.random.normal(streams_of[2], (HD,), jnp.float32), 0.1, 1.9),
        "key_gain": jnp.clip(1.0 + 0.18 * jax.random.normal(streams_of[3], (HD,), jnp.float32), 0.1, 1.9),
        "trainer_qkv": bell_draw(streams_of[4], (D, (HQ + 2 * KVH) * HD), D ** -0.5, 0.125, ((0, 256),), jnp.float32),
        "trainer_gate_up": bell_draw(streams_of[5], (D, 2 * FF), D ** -0.5, 0.125, ((0, 256),), jnp.float32),
        "cache_pages": draw_cache_pages(jax.random.fold_in(streams_of[9], 71), 0),
        "cache_lengths": draw_cache_lengths(jax.random.fold_in(streams_of[9], 71), 0),
        "piece_table": jax.vmap(lambda own: jax.random.permutation(own, SLOTS_G))(jax.random.split(streams_of[8], PROMPTS)).reshape((PROMPTS, SLOTS_G)).astype(jnp.int32),
    }


eps_norm = 1e-06
rope_base = 1000000.0

def rms_scale(values, weight):
    return values * lax.rsqrt(lax.optimization_barrier(jnp.mean(values * values, axis=-1, keepdims=True)) + eps_norm) * weight

def rotate(values, places):
    half_dim = values.shape[-1] // 2
    freqs = rope_base ** (-jnp.arange(half_dim, dtype=jnp.float32) * 2.0 / values.shape[-1])
    angles = places[:, None] * freqs[None, :]
    cosine = jnp.cos(angles)[:, None, :]
    sine = jnp.sin(angles)[:, None, :]
    first = values[..., :half_dim]
    second = values[..., half_dim:]
    return jnp.concatenate([first * cosine - second * sine, second * cosine + first * sine], axis=-1)

def kv_for_blocks(kv_cols, block_count):
    row_count = kv_cols.shape[0]
    by_head = kv_cols.reshape(row_count, KVH, HD)
    if block_count >= KVH:
        return jnp.repeat(by_head, block_count // KVH, axis=1)
    return by_head.reshape(row_count, block_count, KVH // block_count * HD)

def server_layout(trainer_qkv, trainer_gate_up, block_count):
    row_count = trainer_qkv.shape[0]
    query_cols = HQ * HD
    queries = trainer_qkv[:, :query_cols].reshape(row_count, block_count, query_cols // block_count)
    key_part = kv_for_blocks(trainer_qkv[:, query_cols:query_cols + KVH * HD], block_count)
    value_part = kv_for_blocks(trainer_qkv[:, query_cols + KVH * HD:], block_count)
    joined_cols = jnp.concatenate([queries, key_part, value_part], axis=2).reshape(row_count, -1)
    half_cols = trainer_gate_up.shape[1] // 2
    gate_part = trainer_gate_up[:, :half_cols].reshape(row_count, block_count, half_cols // block_count)
    upper_part = trainer_gate_up[:, half_cols:].reshape(row_count, block_count, half_cols // block_count)
    paired_cols = jnp.concatenate([gate_part, upper_part], axis=2).reshape(row_count, -1)
    return (joined_cols.astype(jnp.bfloat16), paired_cols.astype(jnp.bfloat16))

def reference(prompt_states, norm_gain, query_gain, key_gain, trainer_qkv, trainer_gate_up, cache_pages, cache_lengths, piece_table):
    server_qkv, server_gate_up = server_layout(trainer_qkv, trainer_gate_up, N_MP)
    block_idx = np.arange(HQ) // QPD
    local_idx = np.arange(HQ) % QPD // (QPD // KPD)
    kv_of = np.arange(HQ) // (HQ // KVH)
    score_scale = 1.0 / float(np.sqrt(HD))
    token_ids = jnp.arange(PLEN, dtype=jnp.int32)
    causal = token_ids[:, None] >= token_ids[None, :]

    def one_prompt(inputs):
        prompt_rows, cache_block, length, table = inputs
        normed = rms_scale(prompt_rows.astype(jnp.float32), norm_gain).astype(jnp.bfloat16)
        projected = jnp.dot(normed, server_qkv, preferred_element_type=jnp.float32).reshape(PLEN, N_MP, BW)
        queries = projected[:, :, :QPD * HD].reshape(PLEN, HQ, HD)
        key_rows = projected[:, :, QPD * HD:(QPD + KPD) * HD].reshape(PLEN, N_MP * KPD, HD)
        value_rows = projected[:, :, (QPD + KPD) * HD:].reshape(PLEN, N_MP, KPD, HD).astype(jnp.bfloat16)
        places = (length + token_ids).astype(jnp.float32)
        queries = rotate(rms_scale(queries, query_gain), places).astype(jnp.bfloat16)
        key_rows = rotate(rms_scale(key_rows, key_gain), places).astype(jnp.bfloat16).reshape(PLEN, N_MP, KPD, HD)
        self_keys = key_rows[:, block_idx, local_idx]
        self_vals = value_rows[:, block_idx, local_idx]
        flat_cache = cache_block.reshape(SLOTS_G * PIECE, 2, KVH, HD)
        cache_keys = flat_cache[:, 0][:, kv_of]
        cache_vals = flat_cache[:, 1][:, kv_of]
        slot_places = table[:, None] * PIECE + jnp.arange(PIECE, dtype=jnp.int32)[None, :]
        valid = slot_places.reshape(-1) < length

        def one_head(per_head):
            query_h, key_h, val_h, ckey_h, cval_h = per_head
            query_f = query_h.astype(jnp.float32)
            score_self = jnp.dot(query_f, key_h.astype(jnp.float32).T) * score_scale
            score_self = jnp.where(causal, score_self, -1e+30)
            score_cache = jnp.dot(query_f, ckey_h.astype(jnp.float32).T) * score_scale
            score_cache = jnp.where(valid[None, :], score_cache, -1e+30)
            row_max = jnp.maximum(lax.optimization_barrier(jnp.max(score_self, axis=1)), lax.optimization_barrier(jnp.max(score_cache, axis=1)))
            weight_self = jnp.exp(score_self - row_max[:, None])
            weight_cache = jnp.exp(score_cache - row_max[:, None])
            row_total = lax.optimization_barrier(jnp.sum(weight_self, axis=1)) + lax.optimization_barrier(jnp.sum(weight_cache, axis=1))
            summed = jnp.dot(weight_self.astype(jnp.bfloat16).astype(jnp.float32), val_h.astype(jnp.float32))
            summed = summed + jnp.dot(weight_cache.astype(jnp.bfloat16).astype(jnp.float32), cval_h.astype(jnp.float32))
            return summed / row_total[:, None]
        per_head = (jnp.moveaxis(queries, 1, 0), jnp.moveaxis(self_keys, 1, 0), jnp.moveaxis(self_vals, 1, 0), jnp.moveaxis(cache_keys, 1, 0), jnp.moveaxis(cache_vals, 1, 0))
        head_outs = lax.map(one_head, per_head)
        return jnp.moveaxis(head_outs, 0, 1).reshape(PLEN, HQ * HD).astype(jnp.bfloat16)
    attention_out = lax.map(one_prompt, (prompt_states, cache_pages, cache_lengths, piece_table))
    return (server_qkv, server_gate_up, attention_out)
```

```python
import functools

import jax
import jax.numpy as jnp
from jax import lax
from jax.experimental import pallas as pl
from jax.experimental.pallas import tpu as pltpu
from jax.sharding import PartitionSpec as P

HQ = 16
KVH = 8
HD = 128
NX = 4
NZ = 4
NY = 4
NMP = NX * NZ
NDP = 16
PLEN = 1024
PIECE = 512
D = 2048
FF = 6144
NEG = -1e30
EPS = 1e-06
ROPE_BASE = 1000000.0
EXP_SCALE = 1.4426950408889634 / float(HD) ** 0.5
MESH = pl.DeviceIdType.MESH
BF = jnp.bfloat16
F32 = jnp.float32


def rows_of(index, size):
    return pl.ds(pl.multiple_of(index * size, size), size)


class Gather:
    def __init__(self, out_ref, send, recv, dp, mp):
        self.out, self.send, self.recv, self.mp = out_ref, send, recv, mp
        self.c = lax.rem(dp, 2)
        self.y = lax.rem(dp // 2, NY)
        self.zl = dp // (2 * NY)
        self.up = lax.rem(self.y + 1, NY)
        self.down = lax.rem(self.y + NY - 1, NY)
        self.far = lax.rem(self.y + 2, NY)
        self.started = []

    def dp_of(self, zl, y, c):
        return (zl * NY + y) * 2 + c

    def copy(self, slot, block, zl, y, c):
        place = rows_of(block, 128)
        return pltpu.make_async_remote_copy(
            src_ref=self.out.at[place],
            dst_ref=self.out.at[place],
            send_sem=self.send.at[slot],
            recv_sem=self.recv.at[slot],
            device_id=(self.dp_of(zl, y, c), self.mp),
            device_id_type=MESH,
        )

    def go(self, slot, block, zl, y, c):
        one = self.copy(slot, block, zl, y, c)
        one.start()
        self.started.append(one)

    def arrived(self, slot, block):
        self.copy(slot, block, self.zl, self.y, 1 - self.c).wait_recv()

    def to_core(self, slot, block):
        self.go(slot, block, self.zl, self.y, 1 - self.c)

    def run(self):
        zl, y, c, other = self.zl, self.y, self.c, 1 - self.zl
        mine = self.dp_of(zl, y, c)
        pair = self.dp_of(other, y, c)
        self.go(0, mine, other, y, c)
        self.go(1, mine, zl, self.up, c)
        self.go(2, mine, zl, self.down, c)
        self.to_core(7, mine)
        self.arrived(0, pair)
        self.go(3, pair, zl, self.up, c)
        self.go(4, pair, zl, self.down, c)
        self.to_core(8, pair)
        from_down = self.dp_of(zl, self.down, c)
        self.arrived(1, from_down)
        self.go(5, from_down, zl, self.up, c)
        self.to_core(9, from_down)
        from_up = self.dp_of(zl, self.up, c)
        self.arrived(2, from_up)
        self.to_core(10, from_up)
        pair_up = self.dp_of(other, self.up, c)
        self.arrived(4, pair_up)
        self.go(6, pair_up, zl, self.down, c)
        self.to_core(11, pair_up)
        pair_down = self.dp_of(other, self.down, c)
        self.arrived(3, pair_down)
        self.to_core(12, pair_down)
        far = self.dp_of(zl, self.far, c)
        self.arrived(5, far)
        self.to_core(13, far)
        pair_far = self.dp_of(other, self.far, c)
        self.arrived(6, pair_far)
        self.to_core(14, pair_far)

    def finish(self):
        zl, y, c, other = self.zl, self.y, 1 - self.c, 1 - self.zl
        order = (
            (7, zl, y),
            (8, other, y),
            (9, zl, self.down),
            (10, zl, self.up),
            (11, other, self.up),
            (12, other, self.down),
            (13, zl, self.far),
            (14, other, self.far),
        )
        for slot, z_part, y_part in order:
            self.arrived(slot, self.dp_of(z_part, y_part, c))
        for one in self.started:
            one.wait_send()


def greet(dp, mp, gather, with_mp):
    barrier = pltpu.get_barrier_semaphore()
    zl, y, c = gather.zl, gather.y, gather.c
    friends = [
        gather.dp_of(1 - zl, y, c),
        gather.dp_of(zl, gather.up, c),
        gather.dp_of(zl, gather.down, c),
        gather.dp_of(zl, y, 1 - c),
    ]
    for friend in friends:
        pl.semaphore_signal(barrier, inc=1, device_id=(friend, mp), device_id_type=MESH)
    count = len(friends)
    if with_mp:
        for shift in range(1, NMP):
            pl.semaphore_signal(
                barrier, inc=1, device_id=(dp, lax.rem(mp + shift, NMP)), device_id_type=MESH
            )
        count += NMP - 1
    pl.semaphore_wait(barrier, count)


def exchange_kernel(
    qkv_ref, gu_ref, cache_ref, w_ref, g_ref, kv_ref,
    ws, gs, kvtmp, own_sem, w_send, w_recv, g_send, g_recv, kv_send, kv_recv, ag_send, ag_recv,
):
    dp = lax.axis_index("dp")
    mp = lax.axis_index("mp")
    x = mp // NZ
    zh = lax.rem(mp, NZ)
    key_base = HQ * HD
    value_base = key_base + KVH * HD
    for m in range(NMP):
        first = m - m % NZ
        heads = [first + (m % NZ + r) % NZ for r in (1, 2, 3, 0)]
        bases = [h * HD for h in heads]
        bases += [key_base + m // 2 * HD, value_base + m // 2 * HD]
        for slot, base in enumerate(bases):
            ws[m, :, slot * HD : (slot + 1) * HD] = qkv_ref[:, base : base + HD].astype(BF)
        gs[m, :, 0:384] = gu_ref[:, m * 384 : (m + 1) * 384].astype(BF)
        gs[m, :, 384:768] = gu_ref[:, FF + m * 384 : FF + (m + 1) * 384].astype(BF)

    gather = Gather(w_ref, ag_send, ag_recv, dp, mp)
    greet(dp, mp, gather, True)

    sent = []
    home = rows_of(dp * NMP + mp, 8)
    own_w = pltpu.make_async_copy(ws.at[mp], w_ref.at[home], own_sem.at[0])
    own_w.start()
    for shift in range(1, NMP):
        target = lax.rem(mp + shift, NMP)
        one = pltpu.make_async_remote_copy(
            src_ref=ws.at[target], dst_ref=w_ref.at[home],
            send_sem=w_send.at[shift], recv_sem=w_recv.at[shift],
            device_id=(dp, target), device_id_type=MESH,
        )
        one.start()
        sent.append(one)

    kv_copies = []
    for shift in (2, 1, 3):
        there = lax.rem(x + shift, NX)
        for part in range(2):
            cols = pl.ds(pl.multiple_of(part * KVH * HD + there * 256, 256), 256)
            one = pltpu.make_async_remote_copy(
                src_ref=cache_ref.at[:, cols], dst_ref=kv_ref.at[x, part],
                send_sem=kv_send.at[shift * 2 + part], recv_sem=kv_recv.at[shift * 2 + part],
                device_id=(dp, there * NZ + zh), device_id_type=MESH,
            )
            one.start()
            kv_copies.append(one)

    own_kv = []
    for part in range(2):
        cols = pl.ds(pl.multiple_of(part * KVH * HD + x * 256, 256), 256)
        one = pltpu.make_async_copy(cache_ref.at[:, cols], kvtmp.at[part], own_sem.at[1 + part])
        one.start()
        own_kv.append(one)

    own_g = pltpu.make_async_copy(gs.at[mp], g_ref.at[rows_of(mp, 8)], own_sem.at[5])
    own_g.start()
    g_copies = []
    for shift in range(1, NMP):
        target = lax.rem(mp + shift, NMP)
        one = pltpu.make_async_remote_copy(
            src_ref=gs.at[target], dst_ref=g_ref.at[rows_of(mp, 8)],
            send_sem=g_send.at[shift], recv_sem=g_recv.at[shift],
            device_id=(dp, target), device_id_type=MESH,
        )
        one.start()
        g_copies.append(one)

    def from_peer(out_ref, sem, source, place, send):
        return pltpu.make_async_remote_copy(
            src_ref=source, dst_ref=out_ref.at[place], send_sem=send, recv_sem=sem,
            device_id=(dp, lax.rem(mp + 1, NMP)), device_id_type=MESH,
        )

    own_w.wait()
    for shift in range(1, NMP):
        origin = lax.rem(mp + NMP - shift, NMP)
        from_peer(
            w_ref, w_recv.at[shift], ws.at[0], rows_of(dp * NMP + origin, 8), w_send.at[shift]
        ).wait_recv()
    gather.run()

    own_back = []
    for part in range(2):
        own_kv[part].wait()
        one = pltpu.make_async_copy(kvtmp.at[part], kv_ref.at[x, part], own_sem.at[3 + part])
        one.start()
        own_back.append(one)

    gather.finish()
    own_g.wait()
    for shift in range(1, NMP):
        origin = lax.rem(mp + NMP - shift, NMP)
        from_peer(
            g_ref, g_recv.at[shift], gs.at[0], rows_of(origin, 8), g_send.at[shift]
        ).wait_recv()
    for one in own_back:
        one.wait()
    for shift in (2, 1, 3):
        origin = lax.rem(x + NX - shift, NX)
        for part in range(2):
            pltpu.make_async_remote_copy(
                src_ref=kvtmp.at[part], dst_ref=kv_ref.at[origin, part],
                send_sem=kv_send.at[shift * 2 + part], recv_sem=kv_recv.at[shift * 2 + part],
                device_id=(dp, lax.rem(mp + 1, NMP)), device_id_type=MESH,
            ).wait_recv()
    for one in sent + kv_copies + g_copies:
        one.wait_send()


def exchange(trainer_qkv, trainer_gate_up, pages):
    any_space = pl.BlockSpec(memory_space=pl.ANY)
    vmem = pl.BlockSpec(memory_space=pltpu.VMEM)
    dma = pltpu.SemaphoreType.DMA
    return pl.pallas_call(
        exchange_kernel,
        out_shape=(
            jax.ShapeDtypeStruct((D, 768), BF),
            jax.ShapeDtypeStruct((128, 768), BF),
            jax.ShapeDtypeStruct((NX, 2, PIECE, 256), BF),
        ),
        in_specs=[vmem, vmem, any_space],
        out_specs=(any_space, any_space, any_space),
        scratch_shapes=[
            pltpu.VMEM((NMP, 8, 768), BF),
            pltpu.VMEM((NMP, 8, 768), BF),
            pltpu.VMEM((2, PIECE, 256), BF),
            dma((6,)),
            dma((NMP,)), dma((NMP,)), dma((NMP,)), dma((NMP,)),
            dma((8,)), dma((8,)), dma((15,)), dma((15,)),
        ],
        compiler_params=pltpu.CompilerParams(collective_id=0, has_side_effects=True),
        name="exchange",
    )(trainer_qkv, trainer_gate_up, pages)


def spread_kernel(g_ref, after_ref, out_ref, tmp, own_sem, ag_send, ag_recv):
    dp = lax.axis_index("dp")
    mp = lax.axis_index("mp")
    gather = Gather(out_ref, ag_send, ag_recv, dp, mp)
    first = pltpu.make_async_copy(g_ref, tmp, own_sem.at[0])
    first.start()
    first.wait()
    second = pltpu.make_async_copy(tmp, out_ref.at[rows_of(dp, 128)], own_sem.at[1])
    second.start()
    greet(dp, mp, gather, False)
    second.wait()
    gather.run()
    gather.finish()


def spread(block, after):
    any_space = pl.BlockSpec(memory_space=pl.ANY)
    dma = pltpu.SemaphoreType.DMA
    return pl.pallas_call(
        spread_kernel,
        out_shape=jax.ShapeDtypeStruct((D, 768), BF),
        in_specs=[any_space, any_space],
        out_specs=any_space,
        scratch_shapes=[pltpu.VMEM((128, 768), BF), dma((2,)), dma((15,)), dma((15,))],
        compiler_params=pltpu.CompilerParams(collective_id=1, has_side_effects=True),
        name="spread",
    )(block, after)


def project_kernel(x_ref, ng_ref, qg_ref, kg_ref, cos_ref, sin_ref, w_ref, q_ref, k_ref, v_ref):
    rows = x_ref[...].astype(F32)
    mean = jnp.mean(rows * rows, axis=-1, keepdims=True)
    normed = (rows * lax.rsqrt(mean + EPS) * ng_ref[...]).astype(BF)
    projected = jnp.dot(normed, w_ref[...], preferred_element_type=F32)
    cosine = cos_ref[...]
    sine = sin_ref[...]

    def finish(values, gain):
        mean_sq = jnp.mean(values * values, axis=-1, keepdims=True)
        values = values * lax.rsqrt(mean_sq + EPS) * gain
        return (values * cosine + pltpu.roll(values, HD // 2, 1) * sine).astype(BF)

    for slot in range(4):
        q_ref[slot] = finish(projected[:, slot * HD : (slot + 1) * HD], qg_ref[...])
    k_ref[...] = finish(projected[:, 512:640], kg_ref[...])
    v_ref[...] = projected[:, 640:768].astype(BF)


def project(rows, norm_gain, query_gain, key_gain, cosine, sine, weights):
    tile = 256
    whole = lambda shape: pl.BlockSpec(shape, lambda i: (0, 0))
    return pl.pallas_call(
        project_kernel,
        grid=(PLEN // tile,),
        out_shape=(
            jax.ShapeDtypeStruct((4, PLEN, HD), BF),
            jax.ShapeDtypeStruct((PLEN, HD), BF),
            jax.ShapeDtypeStruct((PLEN, HD), BF),
        ),
        in_specs=[
            pl.BlockSpec((tile, D), lambda i: (i, 0)),
            whole((1, D)), whole((1, HD)), whole((1, HD)),
            pl.BlockSpec((tile, HD), lambda i: (i, 0)),
            pl.BlockSpec((tile, HD), lambda i: (i, 0)),
            whole((D, 768)),
        ],
        out_specs=(
            pl.BlockSpec((4, tile, HD), lambda i: (0, i, 0)),
            pl.BlockSpec((tile, HD), lambda i: (i, 0)),
            pl.BlockSpec((tile, HD), lambda i: (i, 0)),
        ),
        cost_estimate=pl.CostEstimate(
            flops=2 * PLEN * D * 768, bytes_accessed=9 * 2**20, transcendentals=0
        ),
        name="project",
    )(rows, norm_gain, query_gain, key_gain, cosine, sine, weights)


def split3(values):
    high = values.astype(BF)
    rest = values - high.astype(F32)
    middle = rest.astype(BF)
    low = (rest - middle.astype(F32)).astype(BF)
    return [high, middle, low]


def contract(left, right, left_dim, right_dim):
    return lax.dot_general(
        left, right, (((left_dim,), (right_dim,)), ((), ())), preferred_element_type=F32
    )


def partial_tile(query, keys, values_t, masks):
    scores = []
    for key, mask in zip(keys, masks):
        score = contract(key, query, 1, 1)
        scores.append(jnp.where(mask, score, NEG) if mask is not None else score)
    top = functools.reduce(jnp.maximum, [jnp.max(s, axis=0, keepdims=True) for s in scores])
    total = 0.0
    summed = 0.0
    for score, value_t in zip(scores, values_t):
        weight = jnp.exp2((score - top) * EXP_SCALE)
        total = total + jnp.sum(weight, axis=0, keepdims=True)
        summed = summed + contract(value_t, weight.astype(BF), 1, 0)
    return top, total, summed


def cache_kernel(info_ref, q_ref, kv_ref, out_ref, vt):
    tile = 256
    column = pl.multiple_of(info_ref[NX] * HD, HD)
    place = lax.broadcasted_iota(jnp.int32, (PIECE, tile), 0)
    masks = [place < info_ref[s] for s in range(NX)]
    for s in range(NX):
        vt[s] = kv_ref[s, 1, :, pl.ds(column, HD)].T

    @pl.loop(0, PLEN // tile)
    def _(t):
        at = pl.multiple_of(t * tile, tile)
        keys = [kv_ref[s, 0, :, pl.ds(column, HD)] for s in range(NX)]
        values_t = [vt[s] for s in range(NX)]
        top, total, summed = partial_tile(q_ref[pl.ds(at, tile), :], keys, values_t, masks)
        out_ref[0:HD, pl.ds(at, tile)] = summed.astype(BF)
        rows = split3(top) + split3(total)
        zero = jnp.zeros((10, tile), F32)
        stats = jnp.concatenate([r.astype(F32) for r in rows] + [zero], axis=0)
        out_ref[HD : HD + 16, pl.ds(at, tile)] = stats.astype(BF)


def cache_part(info, query, kv):
    vmem = pl.BlockSpec(memory_space=pltpu.VMEM)
    return pl.pallas_call(
        cache_kernel,
        out_shape=jax.ShapeDtypeStruct((HD + 16, PLEN), BF),
        in_specs=[pl.BlockSpec(memory_space=pltpu.SMEM), vmem, vmem],
        out_specs=vmem,
        scratch_shapes=[pltpu.VMEM((NX, HD, PIECE), BF)],
        cost_estimate=pl.CostEstimate(
            flops=4 * PLEN * 2048 * HD, bytes_accessed=3 * 2**20, transcendentals=PLEN * 2048
        ),
        name="cache_part",
    )(info, query, kv)


def own_kernel(info_ref, q_ref, k_ref, v_ref, kv_ref, out_ref, st_ref, vt, vs):
    tile = 256
    column = pl.multiple_of(info_ref[NX] * HD, HD)
    place = lax.broadcasted_iota(jnp.int32, (PIECE, tile), 0)
    masks = [place < info_ref[s] for s in range(NX)]
    causal = lax.broadcasted_iota(jnp.int32, (tile, tile), 0) <= lax.broadcasted_iota(
        jnp.int32, (tile, tile), 1
    )
    for s in range(NX):
        vt[s] = kv_ref[s, 1, :, pl.ds(column, HD)].T
    vs[...] = v_ref[...].T
    for t in range(PLEN // tile):
        at = t * tile
        keys = [kv_ref[s, 0, :, pl.ds(column, HD)] for s in range(NX)]
        values_t = [vt[s] for s in range(NX)]
        own_keys = [k_ref[j * tile : (j + 1) * tile, :] for j in range(t + 1)]
        own_values = [vs[:, j * tile : (j + 1) * tile] for j in range(t + 1)]
        own_masks = [None] * t + [causal]
        top, total, summed = partial_tile(
            q_ref[at : at + tile, :], keys + own_keys, values_t + own_values, masks + own_masks
        )
        out_ref[:, at : at + tile] = summed
        st_ref[0:1, at : at + tile] = top
        st_ref[1:2, at : at + tile] = total


def own_part(info, query, key, value, kv):
    vmem = pl.BlockSpec(memory_space=pltpu.VMEM)
    return pl.pallas_call(
        own_kernel,
        out_shape=(
            jax.ShapeDtypeStruct((HD, PLEN), F32),
            jax.ShapeDtypeStruct((8, PLEN), F32),
        ),
        in_specs=[pl.BlockSpec(memory_space=pltpu.SMEM), vmem, vmem, vmem, vmem],
        out_specs=(vmem, vmem),
        scratch_shapes=[pltpu.VMEM((NX, HD, PIECE), BF), pltpu.VMEM((HD, PLEN), BF)],
        cost_estimate=pl.CostEstimate(
            flops=4 * PLEN * 2560 * HD, bytes_accessed=3 * 2**20, transcendentals=PLEN * 2560
        ),
        name="own_part",
    )(info, query, key, value, kv)


def combine_kernel(own_ref, st_ref, a_ref, b_ref, c_ref, out_ref):
    parts = [(own_ref[...], st_ref[0:1, :], st_ref[1:2, :])]
    for ref in (a_ref, b_ref, c_ref):
        stats = ref[HD : HD + 16, :].astype(F32)
        top = stats[0:1] + stats[1:2] + stats[2:3]
        total = stats[3:4] + stats[4:5] + stats[5:6]
        parts.append((ref[0:HD, :].astype(F32), top, total))
    best = functools.reduce(jnp.maximum, [p[1] for p in parts])
    norm = 0.0
    summed = 0.0
    for values, top, total in parts:
        factor = jnp.exp2((top - best) * EXP_SCALE)
        norm = norm + factor * total
        summed = summed + factor * values
    out_ref[...] = (summed / norm).T.astype(BF)


def combine(own, stats, parts):
    return pl.pallas_call(
        combine_kernel,
        out_shape=jax.ShapeDtypeStruct((PLEN, HD), BF),
        in_specs=[pl.BlockSpec(memory_space=pltpu.VMEM)] * 5,
        out_specs=pl.BlockSpec(memory_space=pltpu.VMEM),
        name="combine",
    )(own, stats, *parts)


def per_device(
    prompt_states, norm_gain, query_gain, key_gain, trainer_qkv, trainer_gate_up,
    cache_pages, cache_lengths, piece_table,
):
    mp = lax.axis_index("mp")
    zh = lax.rem(mp, NZ)
    weights, gu_block, kv = exchange(trainer_qkv, trainer_gate_up, cache_pages[0, 0])

    places = (cache_lengths[0] + jnp.arange(PLEN, dtype=jnp.int32)).astype(F32)
    freqs = ROPE_BASE ** (-jnp.arange(HD // 2, dtype=F32) * 2.0 / HD)
    angles = places[:, None] * freqs[None, :]
    cosine = jnp.cos(angles)
    sine = jnp.sin(angles)
    cosine = jnp.concatenate([cosine, cosine], axis=1)
    sine = jnp.concatenate([-sine, sine], axis=1)
    queries, key, value = project(
        prompt_states[0], norm_gain[None], query_gain[None], key_gain[None], cosine, sine, weights
    )

    slots = lax.dynamic_slice_in_dim(piece_table.reshape(NX, NZ), zh, 1, 1)[:, 0]
    visible = jnp.clip(cache_lengths[0] - slots * PIECE, 0, PIECE).astype(jnp.int32)

    def info_of(shift):
        half = lax.rem(zh + shift, NZ) // 2
        return jnp.concatenate([visible, half[None].astype(jnp.int32)])

    arrived = []
    for shift in (2, 1, 3):
        piece = cache_part(info_of(shift), queries[shift - 1], kv)
        perm = [(m, m // NZ * NZ + (m % NZ + shift) % NZ) for m in range(NMP)]
        arrived.append(lax.ppermute(piece, "mp", perm))
    own, stats = own_part(info_of(0), queries[3], key, value, kv)
    gate_block = spread(gu_block, own)
    attended = combine(own, stats, arrived)
    return (weights[:, 384:], gate_block, attended[None])


def solution(mesh):
    placed = (
        P("dp", None, None),
        P(),
        P(),
        P(),
        P(("dp", "mp"), None),
        P(("dp", "mp"), None),
        P("dp", "mp", None, None),
        P("dp"),
        P("dp", None),
    )
    return jax.shard_map(
        per_device,
        mesh=mesh,
        in_specs=placed,
        out_specs=(P(None, "mp"), P(None, "mp"), P("dp", None, "mp")),
        check_vma=False,
    )
```

```python
import functools

import jax
import jax.numpy as jnp
from jax import lax
from jax.experimental import pallas as pl
from jax.experimental.pallas import tpu as pltpu
from jax.sharding import PartitionSpec as P

HQ = 16
KVH = 8
HD = 128
NX = 4
NZ = 4
NY = 4
NMP = NX * NZ
NDP = 16
PLEN = 1024
PIECE = 512
D = 2048
FF = 6144
NEG = -1e30
EPS = 1e-06
ROPE_BASE = 1000000.0
EXP_SCALE = 1.4426950408889634 / float(HD) ** 0.5
MESH = pl.DeviceIdType.MESH
BF = jnp.bfloat16
F32 = jnp.float32


def rows_of(index, size):
    return pl.ds(pl.multiple_of(index * size, size), size)


class Gather:
    def __init__(self, out_ref, send, recv, dp, mp):
        self.out, self.send, self.recv, self.mp = out_ref, send, recv, mp
        self.c = lax.rem(dp, 2)
        self.y = lax.rem(dp // 2, NY)
        self.zl = dp // (2 * NY)
        self.up = lax.rem(self.y + 1, NY)
        self.down = lax.rem(self.y + NY - 1, NY)
        self.far = lax.rem(self.y + 2, NY)
        self.started = []

    def dp_of(self, zl, y, c):
        return (zl * NY + y) * 2 + c

    def copy(self, slot, block, zl, y, c):
        place = rows_of(block, 128)
        return pltpu.make_async_remote_copy(
            src_ref=self.out.at[place],
            dst_ref=self.out.at[place],
            send_sem=self.send.at[slot],
            recv_sem=self.recv.at[slot],
            device_id=(self.dp_of(zl, y, c), self.mp),
            device_id_type=MESH,
        )

    def go(self, slot, block, zl, y, c):
        one = self.copy(slot, block, zl, y, c)
        one.start()
        self.started.append(one)

    def arrived(self, slot, block):
        self.copy(slot, block, self.zl, self.y, 1 - self.c).wait_recv()

    def to_core(self, slot, block):
        self.go(slot, block, self.zl, self.y, 1 - self.c)

    def stages(self):
        zl, y, c, other = self.zl, self.y, self.c, 1 - self.zl
        mine = self.dp_of(zl, y, c)
        pair = self.dp_of(other, y, c)
        self.go(0, mine, other, y, c)
        self.go(1, mine, zl, self.up, c)
        self.go(2, mine, zl, self.down, c)
        self.to_core(7, mine)
        yield
        self.arrived(0, pair)
        self.go(3, pair, zl, self.up, c)
        self.go(4, pair, zl, self.down, c)
        self.to_core(8, pair)
        yield
        from_down = self.dp_of(zl, self.down, c)
        self.arrived(1, from_down)
        self.go(5, from_down, zl, self.up, c)
        self.to_core(9, from_down)
        from_up = self.dp_of(zl, self.up, c)
        self.arrived(2, from_up)
        self.to_core(10, from_up)
        yield
        pair_up = self.dp_of(other, self.up, c)
        self.arrived(4, pair_up)
        self.go(6, pair_up, zl, self.down, c)
        self.to_core(11, pair_up)
        pair_down = self.dp_of(other, self.down, c)
        self.arrived(3, pair_down)
        self.to_core(12, pair_down)
        yield
        far = self.dp_of(zl, self.far, c)
        self.arrived(5, far)
        self.to_core(13, far)
        pair_far = self.dp_of(other, self.far, c)
        self.arrived(6, pair_far)
        self.to_core(14, pair_far)
        yield

    def finish(self):
        zl, y, c, other = self.zl, self.y, 1 - self.c, 1 - self.zl
        order = (
            (7, zl, y),
            (8, other, y),
            (9, zl, self.down),
            (10, zl, self.up),
            (11, other, self.up),
            (12, other, self.down),
            (13, zl, self.far),
            (14, other, self.far),
        )
        for slot, z_part, y_part in order:
            self.arrived(slot, self.dp_of(z_part, y_part, c))
        for one in self.started:
            one.wait_send()


def greet(dp, mp, gather):
    barrier = pltpu.get_barrier_semaphore()
    zl, y, c = gather.zl, gather.y, gather.c
    friends = [
        gather.dp_of(1 - zl, y, c),
        gather.dp_of(zl, gather.up, c),
        gather.dp_of(zl, gather.down, c),
        gather.dp_of(zl, y, 1 - c),
    ]
    for friend in friends:
        pl.semaphore_signal(barrier, inc=1, device_id=(friend, mp), device_id_type=MESH)
    for shift in range(1, NMP):
        pl.semaphore_signal(
            barrier, inc=1, device_id=(dp, lax.rem(mp + shift, NMP)), device_id_type=MESH
        )
    pl.semaphore_wait(barrier, len(friends) + NMP - 1)


def split3(values):
    high = values.astype(BF)
    rest = values - high.astype(F32)
    middle = rest.astype(BF)
    low = (rest - middle.astype(F32)).astype(BF)
    return [high, middle, low]


def contract(left, right, left_dim, right_dim):
    return lax.dot_general(
        left, right, (((left_dim,), (right_dim,)), ((), ())), preferred_element_type=F32
    )


def partial_tile(query, keys, values_t, masks):
    scores = []
    for key, mask in zip(keys, masks):
        score = contract(key, query, 1, 1)
        scores.append(jnp.where(mask, score, NEG) if mask is not None else score)
    top = functools.reduce(jnp.maximum, [jnp.max(s, axis=0, keepdims=True) for s in scores])
    total = 0.0
    summed = 0.0
    for score, value_t in zip(scores, values_t):
        weight = jnp.exp2((score - top) * EXP_SCALE)
        total = total + jnp.sum(weight, axis=0, keepdims=True)
        summed = summed + contract(value_t, weight.astype(BF), 1, 0)
    return top, total, summed


def layer_kernel(
    info_ref, x_ref, ng_ref, qg_ref, kg_ref, cos_ref, sin_ref, qkv_ref, gu_ref, cache_ref,
    w_ref, gate_ref, att_ref,
    ws, gs, xv, wv, kv, kvf, qs, ks, vs, vt, vst, parts, came, partf, own, stat,
    own_sem, w_send, w_recv, g_send, g_recv, kv_send, kv_recv, p_send, p_recv,
    agw_send, agw_recv, agg_send, agg_recv,
):
    dp = lax.axis_index("dp")
    mp = lax.axis_index("mp")
    x = mp // NZ
    zh = lax.rem(mp, NZ)
    key_base = HQ * HD
    value_base = key_base + KVH * HD

    def remote(source, target, send, recv, where):
        return pltpu.make_async_remote_copy(
            src_ref=source, dst_ref=target, send_sem=send, recv_sem=recv,
            device_id=(dp, where), device_id_type=MESH,
        )

    sent = []

    def start(one):
        one.start()
        sent.append(one)

    x_copy = pltpu.make_async_copy(x_ref, xv, own_sem.at[0])
    x_copy.start()
    own_kv = []
    for part in range(2):
        cols = pl.ds(pl.multiple_of(part * KVH * HD + x * 256, 256), 256)
        one = pltpu.make_async_copy(cache_ref.at[:, cols], kv.at[x, part], own_sem.at[1 + part])
        one.start()
        own_kv.append(one)

    for m in range(NMP):
        first = m - m % NZ
        heads = [first + (m % NZ + r) % NZ for r in (1, 2, 3, 0)]
        bases = [h * HD for h in heads]
        bases += [key_base + m // 2 * HD, value_base + m // 2 * HD]
        for slot, base in enumerate(bases):
            ws[m, :, slot * HD : (slot + 1) * HD] = qkv_ref[:, base : base + HD].astype(BF)
        gs[m, :, 0:384] = gu_ref[:, m * 384 : (m + 1) * 384].astype(BF)
        gs[m, :, 384:768] = gu_ref[:, FF + m * 384 : FF + (m + 1) * 384].astype(BF)

    gather_w = Gather(w_ref, agw_send, agw_recv, dp, mp)
    gather_g = Gather(gate_ref, agg_send, agg_recv, dp, mp)
    greet(dp, mp, gather_w)

    home = rows_of(dp * NMP + mp, 8)
    own_w = pltpu.make_async_copy(ws.at[mp], w_ref.at[home], own_sem.at[3])
    own_w.start()
    for shift in range(1, NMP):
        target = lax.rem(mp + shift, NMP)
        start(remote(ws.at[target], w_ref.at[home], w_send.at[shift], w_recv.at[shift], target))

    x_up = lax.rem(x + 1, NX) * NZ + zh
    x_down = lax.rem(x + NX - 1, NX) * NZ + zh
    x_far = lax.rem(x + 2, NX)
    for part, target in enumerate((x_up, x_down)):
        cols = pl.ds(pl.multiple_of(part * KVH * HD + x_far * 256, 256), 256)
        start(remote(
            cache_ref.at[:, cols], kvf.at[part], kv_send.at[part], kv_recv.at[part], target
        ))

    own_g = pltpu.make_async_copy(gs.at[mp], gate_ref.at[home], own_sem.at[4])
    own_g.start()
    for shift in range(1, NMP):
        target = lax.rem(mp + shift, NMP)
        start(remote(gs.at[target], gate_ref.at[home], g_send.at[shift], g_recv.at[shift], target))

    for part in range(2):
        for way, target in enumerate((x_up, x_down)):
            slot = 2 + 2 * way + part
            cols = pl.ds(pl.multiple_of(part * KVH * HD + target // NZ * 256, 256), 256)
            start(remote(
                cache_ref.at[:, cols], kv.at[x, part], kv_send.at[slot], kv_recv.at[slot], target
            ))

    def origin_rows(shift):
        return rows_of(dp * NMP + lax.rem(mp + NMP - shift, NMP), 8)

    own_w.wait()
    for shift in range(1, NMP):
        remote(
            ws.at[0], w_ref.at[origin_rows(shift)], w_send.at[shift], w_recv.at[shift], x_up
        ).wait_recv()
    steps = gather_w.stages()
    next(steps)
    next(steps)
    for part, target in enumerate((x_up, x_down)):
        remote(
            kvf.at[part], kvf.at[part], kv_send.at[part], kv_recv.at[part], target
        ).wait_recv()
        source = lax.rem(x + (NX - 1 if part == 0 else 1), NX)
        start(remote(
            kvf.at[part], kv.at[source, part], kv_send.at[6 + part], kv_recv.at[6 + part], target
        ))
    for _ in steps:
        pass
    own_g.wait()
    for shift in range(1, NMP):
        remote(
            gs.at[0], gate_ref.at[origin_rows(shift)], g_send.at[shift], g_recv.at[shift], x_up
        ).wait_recv()
    steps = gather_g.stages()
    next(steps)
    gather_w.finish()
    w_copy = pltpu.make_async_copy(w_ref, wv, own_sem.at[5])
    w_copy.start()
    x_copy.wait()
    w_copy.wait()

    tile = 256

    def project(at):
        place = pl.ds(at, tile)
        rows = xv[place, :].astype(F32)
        mean = jnp.mean(rows * rows, axis=-1, keepdims=True)
        normed = (rows * lax.rsqrt(mean + EPS) * ng_ref[...]).astype(BF)
        projected = jnp.dot(normed, wv[...], preferred_element_type=F32)
        cosine = cos_ref[place, :]
        sine = sin_ref[place, :]

        def finish(values, gain):
            mean_sq = jnp.mean(values * values, axis=-1, keepdims=True)
            values = values * lax.rsqrt(mean_sq + EPS) * gain
            return (values * cosine + pltpu.roll(values, HD // 2, 1) * sine).astype(BF)

        for slot in range(4):
            qs[slot, place, :] = finish(projected[:, slot * HD : (slot + 1) * HD], qg_ref[...])
        ks[place, :] = finish(projected[:, 512:640], kg_ref[...])
        vs[place, :] = projected[:, 640:768].astype(BF)

    for half in range(2):
        @pl.loop(0, 2)
        def _(t):
            project(pl.multiple_of(half * 512 + t * tile, tile))

        next(steps)

    for part in range(2):
        own_kv[part].wait()
        for slot, source in (
            (2 + part, lax.rem(x + NX - 1, NX)),
            (4 + part, lax.rem(x + 1, NX)),
            (6 + part, x_far),
        ):
            remote(
                kvf.at[part], kv.at[source, part], kv_send.at[slot], kv_recv.at[slot], x_up
            ).wait_recv()

    for half in range(2):
        for s in range(NX):
            vt[half, s] = kv[s, 1, :, half * HD : (half + 1) * HD].T
    vst[...] = vs[...].T

    seat = lax.broadcasted_iota(jnp.int32, (PIECE, tile), 0)
    masks = [seat < info_ref[s] for s in range(NX)]

    def cached(shift):
        half = lax.rem(zh + shift, NZ) // 2
        column = pl.multiple_of(half * HD, HD)
        keys = [kv[s, 0, :, pl.ds(column, HD)] for s in range(NX)]
        return keys, [vt[half, s] for s in range(NX)]

    def cache_part(shift):
        @pl.loop(0, PLEN // tile)
        def _(t):
            at = pl.multiple_of(t * tile, tile)
            keys, values_t = cached(shift)
            query = qs[shift - 1, pl.ds(at, tile), :]
            top, total, summed = partial_tile(query, keys, values_t, masks)
            parts[shift - 1, 0:HD, pl.ds(at, tile)] = summed.astype(BF)
            rows = split3(top) + split3(total)
            zero = jnp.zeros((10, tile), F32)
            stats = jnp.concatenate([r.astype(F32) for r in rows] + [zero], axis=0)
            parts[shift - 1, HD : HD + 16, pl.ds(at, tile)] = stats.astype(BF)

    z_up = x * NZ + lax.rem(zh + 1, NZ)
    z_down = x * NZ + lax.rem(zh + NZ - 1, NZ)
    halves = [(0, z_up), (1, z_down)]

    cache_part(2)
    for half, target in halves:
        start(remote(
            parts.at[1, :, pl.ds(half * 512, 512)], partf.at[half],
            p_send.at[half], p_recv.at[half], target,
        ))
    next(steps)
    cache_part(1)
    start(remote(parts.at[0], came.at[0], p_send.at[4], p_recv.at[4], z_up))
    for half, target in halves:
        remote(
            partf.at[half], partf.at[half], p_send.at[half], p_recv.at[half], target
        ).wait_recv()
        start(remote(
            partf.at[half], came.at[1, :, pl.ds(half * 512, 512)],
            p_send.at[2 + half], p_recv.at[2 + half], target,
        ))
    cache_part(3)
    start(remote(parts.at[2], came.at[2], p_send.at[5], p_recv.at[5], z_down))
    for _ in steps:
        pass

    causal = lax.broadcasted_iota(jnp.int32, (tile, tile), 0) <= lax.broadcasted_iota(
        jnp.int32, (tile, tile), 1
    )
    for t in range(PLEN // tile):
        at = t * tile
        keys, values_t = cached(0)
        own_keys = [ks[j * tile : (j + 1) * tile, :] for j in range(t + 1)]
        own_values = [vst[:, j * tile : (j + 1) * tile] for j in range(t + 1)]
        own_masks = [None] * t + [causal]
        top, total, summed = partial_tile(
            qs[3, at : at + tile, :], keys + own_keys, values_t + own_values, masks + own_masks
        )
        own[:, at : at + tile] = summed
        stat[0:1, at : at + tile] = top
        stat[1:2, at : at + tile] = total

    for half, target in halves:
        remote(
            partf.at[half], came.at[1, :, pl.ds(half * 512, 512)],
            p_send.at[2 + half], p_recv.at[2 + half], target,
        ).wait_recv()
    remote(parts.at[0], came.at[0], p_send.at[4], p_recv.at[4], z_up).wait_recv()
    remote(parts.at[2], came.at[2], p_send.at[5], p_recv.at[5], z_down).wait_recv()

    for t in range(PLEN // tile):
        place = slice(t * tile, (t + 1) * tile)
        pieces = [(own[:, place], stat[0:1, place], stat[1:2, place])]
        for i in range(3):
            stats = came[i, HD : HD + 16, place].astype(F32)
            top = stats[0:1] + stats[1:2] + stats[2:3]
            total = stats[3:4] + stats[4:5] + stats[5:6]
            pieces.append((came[i, 0:HD, place].astype(F32), top, total))
        best = functools.reduce(jnp.maximum, [p[1] for p in pieces])
        norm = 0.0
        summed = 0.0
        for values, top, total in pieces:
            factor = jnp.exp2((top - best) * EXP_SCALE)
            norm = norm + factor * total
            summed = summed + factor * values
        att_ref[place, :] = (summed / norm).T.astype(BF)

    gather_g.finish()
    for one in sent:
        one.wait_send()


def layer(info, rows, norm_gain, query_gain, key_gain, cosine, sine, qkv, gate_up, pages):
    any_space = pl.BlockSpec(memory_space=pl.ANY)
    vmem = pl.BlockSpec(memory_space=pltpu.VMEM)
    dma = pltpu.SemaphoreType.DMA
    return pl.pallas_call(
        layer_kernel,
        out_shape=(
            jax.ShapeDtypeStruct((D, 768), BF),
            jax.ShapeDtypeStruct((D, 768), BF),
            jax.ShapeDtypeStruct((PLEN, HD), BF),
        ),
        in_specs=[
            pl.BlockSpec(memory_space=pltpu.SMEM), any_space,
            vmem, vmem, vmem, vmem, vmem, vmem, vmem, any_space,
        ],
        out_specs=(any_space, any_space, vmem),
        scratch_shapes=[
            pltpu.VMEM((NMP, 8, 768), BF),
            pltpu.VMEM((NMP, 8, 768), BF),
            pltpu.VMEM((PLEN, D), BF),
            pltpu.VMEM((D, 768), BF),
            pltpu.VMEM((NX, 2, PIECE, 256), BF),
            pltpu.VMEM((2, PIECE, 256), BF),
            pltpu.VMEM((4, PLEN, HD), BF),
            pltpu.VMEM((PLEN, HD), BF),
            pltpu.VMEM((PLEN, HD), BF),
            pltpu.VMEM((2, NX, HD, PIECE), BF),
            pltpu.VMEM((HD, PLEN), BF),
            pltpu.VMEM((3, HD + 16, PLEN), BF),
            pltpu.VMEM((3, HD + 16, PLEN), BF),
            pltpu.VMEM((2, HD + 16, PLEN // 2), BF),
            pltpu.VMEM((HD, PLEN), F32),
            pltpu.VMEM((8, PLEN), F32),
            dma((6,)),
            dma((NMP,)), dma((NMP,)), dma((NMP,)), dma((NMP,)),
            dma((8,)), dma((8,)), dma((6,)), dma((6,)),
            dma((15,)), dma((15,)), dma((15,)), dma((15,)),
        ],
        compiler_params=pltpu.CompilerParams(
            collective_id=0, has_side_effects=True, vmem_limit_bytes=56 * 2**20
        ),
        name="layer",
    )(info, rows, norm_gain, query_gain, key_gain, cosine, sine, qkv, gate_up, pages)


def per_device(
    prompt_states, norm_gain, query_gain, key_gain, trainer_qkv, trainer_gate_up,
    cache_pages, cache_lengths, piece_table,
):
    zh = lax.rem(lax.axis_index("mp"), NZ)
    places = (cache_lengths[0] + jnp.arange(PLEN, dtype=jnp.int32)).astype(F32)
    freqs = ROPE_BASE ** (-jnp.arange(HD // 2, dtype=F32) * 2.0 / HD)
    angles = places[:, None] * freqs[None, :]
    cosine = jnp.cos(angles)
    sine = jnp.sin(angles)
    cosine = jnp.concatenate([cosine, cosine], axis=1)
    sine = jnp.concatenate([-sine, sine], axis=1)
    slots = lax.dynamic_slice_in_dim(piece_table.reshape(NX, NZ), zh, 1, 1)[:, 0]
    visible = jnp.clip(cache_lengths[0] - slots * PIECE, 0, PIECE).astype(jnp.int32)
    weights, gate_block, attended = layer(
        visible, prompt_states[0], norm_gain[None], query_gain[None], key_gain[None],
        cosine, sine, trainer_qkv, trainer_gate_up, cache_pages[0, 0],
    )
    return (weights[:, 384:], gate_block, attended[None])


def solution(mesh):
    placed = (
        P("dp", None, None),
        P(),
        P(),
        P(),
        P(("dp", "mp"), None),
        P(("dp", "mp"), None),
        P("dp", "mp", None, None),
        P("dp"),
        P("dp", None),
    )
    return jax.shard_map(
        per_device,
        mesh=mesh,
        in_specs=placed,
        out_specs=(P(None, "mp"), P(None, "mp"), P("dp", None, "mp")),
        check_vma=False,
    )
```

```python
import functools

import jax
import numpy as np
import jax.numpy as jnp
from jax import lax
from jax.experimental import pallas as pl
from jax.experimental.pallas import tpu as pltpu
from jax.sharding import PartitionSpec as P

HQ = 16
KVH = 8
HD = 128
NX = 4
NZ = 4
NY = 4
NMP = NX * NZ
NDP = 16
PLEN = 1024
PIECE = 512
D = 2048
FF = 6144
NEG = -1e30
EPS = 1e-06
ROPE_BASE = 1000000.0
EXP_SCALE = 1.4426950408889634 / float(HD) ** 0.5
MESH = pl.DeviceIdType.MESH
BF = jnp.bfloat16
F32 = jnp.float32


def rows_of(index, size):
    return pl.ds(pl.multiple_of(index * size, size), size)


class Gather:
    def __init__(self, out_ref, send, recv, dp, mp):
        self.out, self.send, self.recv, self.mp = out_ref, send, recv, mp
        self.c = lax.rem(dp, 2)
        self.y = lax.rem(dp // 2, NY)
        self.zl = dp // (2 * NY)
        self.up = lax.rem(self.y + 1, NY)
        self.down = lax.rem(self.y + NY - 1, NY)
        self.far = lax.rem(self.y + 2, NY)
        self.started = []

    def dp_of(self, zl, y, c):
        return (zl * NY + y) * 2 + c

    def copy(self, slot, block, zl, y, c):
        place = rows_of(block, 128)
        return pltpu.make_async_remote_copy(
            src_ref=self.out.at[place],
            dst_ref=self.out.at[place],
            send_sem=self.send.at[slot],
            recv_sem=self.recv.at[slot],
            device_id=(self.dp_of(zl, y, c), self.mp),
            device_id_type=MESH,
        )

    def go(self, slot, block, zl, y, c):
        one = self.copy(slot, block, zl, y, c)
        one.start()
        self.started.append(one)

    def arrived(self, slot, block):
        self.copy(slot, block, self.zl, self.y, 1 - self.c).wait_recv()

    def to_core(self, slot, block):
        self.go(slot, block, self.zl, self.y, 1 - self.c)

    def stages(self):
        zl, y, c, other = self.zl, self.y, self.c, 1 - self.zl
        mine = self.dp_of(zl, y, c)
        pair = self.dp_of(other, y, c)
        self.go(0, mine, other, y, c)
        self.go(1, mine, zl, self.up, c)
        self.go(2, mine, zl, self.down, c)
        self.to_core(7, mine)
        yield
        self.arrived(0, pair)
        self.go(3, pair, zl, self.up, c)
        self.go(4, pair, zl, self.down, c)
        self.to_core(8, pair)
        yield
        from_down = self.dp_of(zl, self.down, c)
        self.arrived(1, from_down)
        self.go(5, from_down, zl, self.up, c)
        self.to_core(9, from_down)
        from_up = self.dp_of(zl, self.up, c)
        self.arrived(2, from_up)
        self.to_core(10, from_up)
        yield
        pair_up = self.dp_of(other, self.up, c)
        self.arrived(4, pair_up)
        self.go(6, pair_up, zl, self.down, c)
        self.to_core(11, pair_up)
        pair_down = self.dp_of(other, self.down, c)
        self.arrived(3, pair_down)
        self.to_core(12, pair_down)
        yield
        far = self.dp_of(zl, self.far, c)
        self.arrived(5, far)
        self.to_core(13, far)
        pair_far = self.dp_of(other, self.far, c)
        self.arrived(6, pair_far)
        self.to_core(14, pair_far)
        yield

    def finish(self):
        zl, y, c, other = self.zl, self.y, 1 - self.c, 1 - self.zl
        order = (
            (7, zl, y),
            (8, other, y),
            (9, zl, self.down),
            (10, zl, self.up),
            (11, other, self.up),
            (12, other, self.down),
            (13, zl, self.far),
            (14, other, self.far),
        )
        for slot, z_part, y_part in order:
            self.arrived(slot, self.dp_of(z_part, y_part, c))
        for one in self.started:
            one.wait_send()


def greet(dp, mp, gather):
    barrier = pltpu.get_barrier_semaphore()
    zl, y, c = gather.zl, gather.y, gather.c
    friends = [
        gather.dp_of(1 - zl, y, c),
        gather.dp_of(zl, gather.up, c),
        gather.dp_of(zl, gather.down, c),
        gather.dp_of(zl, y, 1 - c),
    ]
    for friend in friends:
        pl.semaphore_signal(barrier, inc=1, device_id=(friend, mp), device_id_type=MESH)
    for shift in range(1, NMP):
        pl.semaphore_signal(
            barrier, inc=1, device_id=(dp, lax.rem(mp + shift, NMP)), device_id_type=MESH
        )
    pl.semaphore_wait(barrier, len(friends) + NMP - 1)


def split3(values):
    high = values.astype(BF)
    rest = values - high.astype(F32)
    middle = rest.astype(BF)
    low = (rest - middle.astype(F32)).astype(BF)
    return [high, middle, low]


def contract(left, right, left_dim, right_dim):
    return lax.dot_general(
        left, right, (((left_dim,), (right_dim,)), ((), ())), preferred_element_type=F32
    )


def partial_tile(query, keys, values_t, masks):
    scores = []
    for key, mask in zip(keys, masks):
        score = contract(key, query, 1, 1)
        scores.append(jnp.where(mask, score, NEG) if mask is not None else score)
    top = functools.reduce(jnp.maximum, [jnp.max(s, axis=0, keepdims=True) for s in scores])
    total = 0.0
    summed = 0.0
    for score, value_t in zip(scores, values_t):
        weight = jnp.exp2((score - top) * EXP_SCALE)
        total = total + jnp.sum(weight, axis=0, keepdims=True)
        summed = summed + contract(value_t, weight.astype(BF), 1, 0)
    return top, total, summed


def layer_kernel(
    len_ref, table_ref, x_ref, ng_ref, qg_ref, kg_ref, freq_ref, qkv_ref, gu_ref, cache_ref,
    sqkv_ref, gate_ref, att_ref,
    cos_ref, sin_ref, ws, gs, xv, wv, kv, kvf, qs, ks, vs, vt, vst, parts, came, partf, own, stat,
    own_sem, w_send, w_recv, g_send, g_recv, kv_send, kv_recv, p_send, p_recv,
    agw_send, agw_recv, agg_send, agg_recv,
):
    dp = lax.axis_index("dp")
    mp = lax.axis_index("mp")
    x = mp // NZ
    zh = lax.rem(mp, NZ)
    key_base = HQ * HD
    value_base = key_base + KVH * HD

    def remote(source, target, send, recv, where):
        return pltpu.make_async_remote_copy(
            src_ref=source, dst_ref=target, send_sem=send, recv_sem=recv,
            device_id=(dp, where), device_id_type=MESH,
        )

    sent = []

    def start(one):
        one.start()
        sent.append(one)

    x_copy = pltpu.make_async_copy(x_ref, xv, own_sem.at[0])
    x_copy.start()
    own_kv = []
    for part in range(2):
        cols = pl.ds(pl.multiple_of(part * KVH * HD + x * 256, 256), 256)
        one = pltpu.make_async_copy(cache_ref.at[:, cols], kv.at[x, part], own_sem.at[1 + part])
        one.start()
        own_kv.append(one)

    for m in range(NMP):
        first = m - m % NZ
        heads = [first + (m % NZ + r) % NZ for r in (1, 2, 3, 0)]
        bases = [h * HD for h in heads]
        bases += [key_base + m // 2 * HD, value_base + m // 2 * HD]
        for slot, base in enumerate(bases):
            ws[m, :, slot * HD : (slot + 1) * HD] = qkv_ref[:, base : base + HD].astype(BF)
        gs[m, :, 0:384] = gu_ref[:, m * 384 : (m + 1) * 384].astype(BF)
        gs[m, :, 384:768] = gu_ref[:, FF + m * 384 : FF + (m + 1) * 384].astype(BF)

    gather_w = Gather(wv, agw_send, agw_recv, dp, mp)
    gather_g = Gather(gate_ref, agg_send, agg_recv, dp, mp)
    greet(dp, mp, gather_w)

    home = rows_of(dp * NMP + mp, 8)
    own_w = pltpu.make_async_copy(ws.at[mp], wv.at[home], own_sem.at[3])
    own_w.start()
    for shift in range(1, NMP):
        target = lax.rem(mp + shift, NMP)
        start(remote(ws.at[target], wv.at[home], w_send.at[shift], w_recv.at[shift], target))

    x_up = lax.rem(x + 1, NX) * NZ + zh
    x_down = lax.rem(x + NX - 1, NX) * NZ + zh
    x_far = lax.rem(x + 2, NX)
    for part, target in enumerate((x_up, x_down)):
        cols = pl.ds(pl.multiple_of(part * KVH * HD + x_far * 256, 256), 256)
        start(remote(
            cache_ref.at[:, cols], kvf.at[part], kv_send.at[part], kv_recv.at[part], target
        ))

    own_g = pltpu.make_async_copy(gs.at[mp], gate_ref.at[home], own_sem.at[4])
    own_g.start()
    for shift in range(1, NMP):
        target = lax.rem(mp + shift, NMP)
        start(remote(gs.at[target], gate_ref.at[home], g_send.at[shift], g_recv.at[shift], target))

    for part in range(2):
        for way, target in enumerate((x_up, x_down)):
            slot = 2 + 2 * way + part
            cols = pl.ds(pl.multiple_of(part * KVH * HD + target // NZ * 256, 256), 256)
            start(remote(
                cache_ref.at[:, cols], kv.at[x, part], kv_send.at[slot], kv_recv.at[slot], target
            ))

    def origin_rows(shift):
        return rows_of(dp * NMP + lax.rem(mp + NMP - shift, NMP), 8)

    length = len_ref[0]
    span = 32
    freq = freq_ref[...]
    row = lax.broadcasted_iota(jnp.int32, (span, HD), 0)
    coarse = (length + row * span).astype(F32) * freq
    fine = row.astype(F32) * freq
    sign = jnp.where(lax.broadcasted_iota(jnp.int32, (1, HD), 1) < HD // 2, -1.0, 1.0)
    cos_a, sin_a, cos_b, sin_b = jnp.cos(coarse), jnp.sin(coarse), jnp.cos(fine), jnp.sin(fine)
    for a in range(PLEN // span):
        ca, sa = cos_a[a : a + 1], sin_a[a : a + 1]
        cos_ref[a * span : (a + 1) * span, :] = ca * cos_b - sa * sin_b
        sin_ref[a * span : (a + 1) * span, :] = (sa * cos_b + ca * sin_b) * sign

    own_w.wait()
    for shift in range(1, NMP):
        remote(
            ws.at[0], wv.at[origin_rows(shift)], w_send.at[shift], w_recv.at[shift], x_up
        ).wait_recv()
    steps = gather_w.stages()
    next(steps)
    next(steps)
    for part, target in enumerate((x_up, x_down)):
        remote(
            kvf.at[part], kvf.at[part], kv_send.at[part], kv_recv.at[part], target
        ).wait_recv()
        source = lax.rem(x + (NX - 1 if part == 0 else 1), NX)
        start(remote(
            kvf.at[part], kv.at[source, part], kv_send.at[6 + part], kv_recv.at[6 + part], target
        ))
    for _ in steps:
        pass
    own_g.wait()
    for shift in range(1, NMP):
        remote(
            gs.at[0], gate_ref.at[origin_rows(shift)], g_send.at[shift], g_recv.at[shift], x_up
        ).wait_recv()
    steps = gather_g.stages()
    next(steps)
    gather_w.finish()
    w_copy = pltpu.make_async_copy(wv.at[:, pl.ds(384, 384)], sqkv_ref, own_sem.at[5])
    w_copy.start()
    x_copy.wait()

    tile = 256

    def project(at):
        place = pl.ds(at, tile)
        rows = xv[place, :].astype(F32)
        mean = jnp.mean(rows * rows, axis=-1, keepdims=True)
        normed = (rows * lax.rsqrt(mean + EPS) * ng_ref[...]).astype(BF)
        projected = jnp.dot(normed, wv[...], preferred_element_type=F32)
        cosine = cos_ref[place, :]
        sine = sin_ref[place, :]

        def finish(values, gain):
            mean_sq = jnp.mean(values * values, axis=-1, keepdims=True)
            values = values * lax.rsqrt(mean_sq + EPS) * gain
            return (values * cosine + pltpu.roll(values, HD // 2, 1) * sine).astype(BF)

        for slot in range(4):
            qs[slot, place, :] = finish(projected[:, slot * HD : (slot + 1) * HD], qg_ref[...])
        ks[place, :] = finish(projected[:, 512:640], kg_ref[...])
        vs[place, :] = projected[:, 640:768].astype(BF)

    for half in range(2):
        @pl.loop(0, 2)
        def _(t):
            project(pl.multiple_of(half * 512 + t * tile, tile))

        next(steps)

    for part in range(2):
        own_kv[part].wait()
        for slot, source in (
            (2 + part, lax.rem(x + NX - 1, NX)),
            (4 + part, lax.rem(x + 1, NX)),
            (6 + part, x_far),
        ):
            remote(
                kvf.at[part], kv.at[source, part], kv_send.at[slot], kv_recv.at[slot], x_up
            ).wait_recv()

    for half in range(2):
        for s in range(NX):
            vt[half, s] = kv[s, 1, :, half * HD : (half + 1) * HD].T
    vst[...] = vs[...].T

    seat = lax.broadcasted_iota(jnp.int32, (PIECE, tile), 0)
    masks = [seat < length - table_ref[0, s * NZ + zh] * PIECE for s in range(NX)]

    def cached(shift):
        half = lax.rem(zh + shift, NZ) // 2
        column = pl.multiple_of(half * HD, HD)
        keys = [kv[s, 0, :, pl.ds(column, HD)] for s in range(NX)]
        return keys, [vt[half, s] for s in range(NX)]

    def cache_part(shift):
        @pl.loop(0, PLEN // tile)
        def _(t):
            at = pl.multiple_of(t * tile, tile)
            keys, values_t = cached(shift)
            query = qs[shift - 1, pl.ds(at, tile), :]
            top, total, summed = partial_tile(query, keys, values_t, masks)
            parts[shift - 1, 0:HD, pl.ds(at, tile)] = summed.astype(BF)
            rows = split3(top) + split3(total)
            zero = jnp.zeros((10, tile), F32)
            stats = jnp.concatenate([r.astype(F32) for r in rows] + [zero], axis=0)
            parts[shift - 1, HD : HD + 16, pl.ds(at, tile)] = stats.astype(BF)

    z_up = x * NZ + lax.rem(zh + 1, NZ)
    z_down = x * NZ + lax.rem(zh + NZ - 1, NZ)
    halves = [(0, z_up), (1, z_down)]

    cache_part(2)
    for half, target in halves:
        start(remote(
            parts.at[1, :, pl.ds(half * 512, 512)], partf.at[half],
            p_send.at[half], p_recv.at[half], target,
        ))
    next(steps)
    cache_part(1)
    start(remote(parts.at[0], came.at[0], p_send.at[4], p_recv.at[4], z_up))
    for half, target in halves:
        remote(
            partf.at[half], partf.at[half], p_send.at[half], p_recv.at[half], target
        ).wait_recv()
        start(remote(
            partf.at[half], came.at[1, :, pl.ds(half * 512, 512)],
            p_send.at[2 + half], p_recv.at[2 + half], target,
        ))
    cache_part(3)
    start(remote(parts.at[2], came.at[2], p_send.at[5], p_recv.at[5], z_down))
    for _ in steps:
        pass

    causal = lax.broadcasted_iota(jnp.int32, (tile, tile), 0) <= lax.broadcasted_iota(
        jnp.int32, (tile, tile), 1
    )
    for t in range(PLEN // tile):
        at = t * tile
        keys, values_t = cached(0)
        own_keys = [ks[j * tile : (j + 1) * tile, :] for j in range(t + 1)]
        own_values = [vst[:, j * tile : (j + 1) * tile] for j in range(t + 1)]
        own_masks = [None] * t + [causal]
        top, total, summed = partial_tile(
            qs[3, at : at + tile, :], keys + own_keys, values_t + own_values, masks + own_masks
        )
        own[:, at : at + tile] = summed
        stat[0:1, at : at + tile] = top
        stat[1:2, at : at + tile] = total

    for half, target in halves:
        remote(
            partf.at[half], came.at[1, :, pl.ds(half * 512, 512)],
            p_send.at[2 + half], p_recv.at[2 + half], target,
        ).wait_recv()
    remote(parts.at[0], came.at[0], p_send.at[4], p_recv.at[4], z_up).wait_recv()
    remote(parts.at[2], came.at[2], p_send.at[5], p_recv.at[5], z_down).wait_recv()

    for t in range(PLEN // tile):
        place = slice(t * tile, (t + 1) * tile)
        pieces = [(own[:, place], stat[0:1, place], stat[1:2, place])]
        for i in range(3):
            stats = came[i, HD : HD + 16, place].astype(F32)
            top = stats[0:1] + stats[1:2] + stats[2:3]
            total = stats[3:4] + stats[4:5] + stats[5:6]
            pieces.append((came[i, 0:HD, place].astype(F32), top, total))
        best = functools.reduce(jnp.maximum, [p[1] for p in pieces])
        norm = 0.0
        summed = 0.0
        for values, top, total in pieces:
            factor = jnp.exp2((top - best) * EXP_SCALE)
            norm = norm + factor * total
            summed = summed + factor * values
        att_ref[place, :] = (summed / norm).T.astype(BF)

    w_copy.wait()
    gather_g.finish()
    for one in sent:
        one.wait_send()


def layer(lengths, table, rows, norm_gain, query_gain, key_gain, freqs, qkv, gate_up, pages):
    any_space = pl.BlockSpec(memory_space=pl.ANY)
    vmem = pl.BlockSpec(memory_space=pltpu.VMEM)
    dma = pltpu.SemaphoreType.DMA
    return pl.pallas_call(
        layer_kernel,
        out_shape=(
            jax.ShapeDtypeStruct((D, 384), BF),
            jax.ShapeDtypeStruct((D, 768), BF),
            jax.ShapeDtypeStruct((PLEN, HD), BF),
        ),
        in_specs=[
            pl.BlockSpec(memory_space=pltpu.SMEM), pl.BlockSpec(memory_space=pltpu.SMEM), any_space,
            vmem, vmem, vmem, vmem, vmem, vmem, any_space,
        ],
        out_specs=(any_space, any_space, vmem),
        scratch_shapes=[
            pltpu.VMEM((PLEN, HD), F32),
            pltpu.VMEM((PLEN, HD), F32),
            pltpu.VMEM((NMP, 8, 768), BF),
            pltpu.VMEM((NMP, 8, 768), BF),
            pltpu.VMEM((PLEN, D), BF),
            pltpu.VMEM((D, 768), BF),
            pltpu.VMEM((NX, 2, PIECE, 256), BF),
            pltpu.VMEM((2, PIECE, 256), BF),
            pltpu.VMEM((4, PLEN, HD), BF),
            pltpu.VMEM((PLEN, HD), BF),
            pltpu.VMEM((PLEN, HD), BF),
            pltpu.VMEM((2, NX, HD, PIECE), BF),
            pltpu.VMEM((HD, PLEN), BF),
            pltpu.VMEM((3, HD + 16, PLEN), BF),
            pltpu.VMEM((3, HD + 16, PLEN), BF),
            pltpu.VMEM((2, HD + 16, PLEN // 2), BF),
            pltpu.VMEM((HD, PLEN), F32),
            pltpu.VMEM((8, PLEN), F32),
            dma((6,)),
            dma((NMP,)), dma((NMP,)), dma((NMP,)), dma((NMP,)),
            dma((8,)), dma((8,)), dma((6,)), dma((6,)),
            dma((15,)), dma((15,)), dma((15,)), dma((15,)),
        ],
        compiler_params=pltpu.CompilerParams(
            collective_id=0, has_side_effects=True, vmem_limit_bytes=56 * 2**20
        ),
        name="layer",
    )(lengths, table, rows, norm_gain, query_gain, key_gain, freqs, qkv, gate_up, pages)


def per_device(
    prompt_states, norm_gain, query_gain, key_gain, trainer_qkv, trainer_gate_up,
    cache_pages, cache_lengths, piece_table,
):
    half = ROPE_BASE ** (-np.arange(HD // 2) * 2.0 / HD)
    freqs = jnp.asarray(np.concatenate([half, half])[None], F32)
    server_qkv, gate_block, attended = layer(
        cache_lengths, piece_table, prompt_states[0], norm_gain[None], query_gain[None],
        key_gain[None], freqs, trainer_qkv, trainer_gate_up, cache_pages[0, 0],
    )
    return (server_qkv, gate_block, attended[None])


def solution(mesh):
    placed = (
        P("dp", None, None),
        P(),
        P(),
        P(),
        P(("dp", "mp"), None),
        P(("dp", "mp"), None),
        P("dp", "mp", None, None),
        P("dp"),
        P("dp", None),
    )
    return jax.shard_map(
        per_device,
        mesh=mesh,
        in_specs=placed,
        out_specs=(P(None, "mp"), P(None, "mp"), P("dp", None, "mp")),
        check_vma=False,
    )
```
